512 devices in a mesh: rows: 64 (over z, x), samp: 8 (over y, core).
Axes of the slice: x: 4, y: 4, z: 16, core: 2. Of those that a mesh axis runs over, the one named last changes fastest.
Arguments:
- sketch: float32 [256, 786432], P('samp', 'rows'), may hold values from -6 to 6
- probes: float32 [256, 786432], P('samp', 'rows'), may hold values from -6 to 6
- test_leaf: float32 [64, 256], replicated, may hold values from -0.375 to 0.375
- test_parent: float32 [64, 256], replicated, may hold values from -0.375 to 0.375
- leaf_far: int32 [3072, 8], P(('rows', 'samp')), may hold values from 0 to 3071, as said below
- leaf_count: int32 [3072], P(('rows', 'samp')), may hold values from 1 to 8
- parent_far: int32 [1536, 8], P(('rows', 'samp')), may hold values from 0 to 1535, as said below
- parent_count: int32 [1536], P(('rows', 'samp')), may hold values from 1 to 8
Outputs:
- leaf_basis: float32 [64, 786432], P(None, ('rows', 'samp'))
- leaf_coupling: float32 [3072, 8, 4096], P(('rows', 'samp'))
- transfer: float32 [1536, 64, 128], P(('rows', 'samp'))
- parent_coupling: float32 [1536, 8, 4096], P(('rows', 'samp'))
The draws below stay inside these ranges and needn't reach their ends.
Inputs may be any that keep to these rules, and one draw needn't show every extreme that they name: leaf_far[i, k] = j satisfies 2 <= |i - j| <= 6. `parent_far`: with b(p) = p // 3, a partner q of p has b(q) - b(p) a nonzero multiple of 8, at most 4 * 8 in magnitude.
All inputs are finite; a program needn't handle non-finite values.
Results may differ from the reference program's by a relative error of at most 0.0041.
Values may be sent and summed in bfloat16 or wider, within the bound.
No kernel may reach another device: no remote copies, remote signals or barrier semaphores. Data moves between devices by JAX's collectives and lax.ppermute only.
A program may use at most 64 MiB of HBM per device.

```python
import jax
import jax.numpy as jnp
from jax import lax

LEAF = 256
RANK = 64
SAMPLES = 256
NFAR = 8
REACH = 4
LEAF_DEV = 6
LEAVES = 3072
PARENTS = 1536
ORDER = 786432
N_ROWS = 64
N_SAMP = 8


def draw_leaf_far(key, part):
    first_key, second_key = jax.random.split(jax.random.fold_in(key, 11))
    leaf_ids = jnp.arange(LEAVES, dtype=jnp.int32)[:, None]
    distance = 2 + jax.random.randint(first_key, (LEAVES, NFAR), 0, LEAF_DEV - 1)
    direction = jax.random.randint(second_key, (LEAVES, NFAR), 0, 2) * 2 - 1
    partner = leaf_ids + direction * distance
    outside = (partner < 0) | (partner >= LEAVES)
    partner = jnp.where(outside, leaf_ids - direction * distance, partner)
    return partner.astype(jnp.int32)


def draw_leaf_count(key, part):
    return jax.random.randint(jax.random.fold_in(key, 23), (LEAVES,), 1, NFAR + 1).astype(jnp.int32)


def draw_parent_far(key, part):
    first_key, second_key, third_key = jax.random.split(jax.random.fold_in(key, 37), 3)
    per_device = LEAF_DEV // 2
    parent_ids = jnp.arange(PARENTS, dtype=jnp.int32)[:, None]
    block_ids = parent_ids // per_device
    row_ids = block_ids // N_SAMP
    column_ids = block_ids % N_SAMP
    distance = 1 + jax.random.randint(first_key, (PARENTS, NFAR), 0, REACH)
    direction = jax.random.randint(second_key, (PARENTS, NFAR), 0, 2) * 2 - 1
    target_row = row_ids + direction * distance
    outside = (target_row < 0) | (target_row >= N_ROWS)
    target_row = jnp.where(outside, row_ids - direction * distance, target_row)
    within = jax.random.randint(third_key, (PARENTS, NFAR), 0, per_device)
    partner = (target_row * N_SAMP + column_ids) * per_device + within
    return partner.astype(jnp.int32)


def draw_parent_count(key, part):
    return jax.random.randint(jax.random.fold_in(key, 41), (PARENTS,), 1, NFAR + 1).astype(jnp.int32)


def shard_levels(own_key, extent, shards, least, top_value):
    def one(dim, shards_of):
        draws = jax.random.uniform(jax.random.fold_in(jax.random.fold_in(own_key, 6), dim), (shards_of,), jnp.float32, least / len(shards), top_value / len(shards))
        return jnp.repeat(jnp.exp(draws), extent[dim] // shards_of).reshape((-1,) + (1,) * (len(extent) - dim - 1))

    level = one(*shards[0])
    for cut in shards[1:]:
        level = level * one(*cut)
    return level


def gaussian(own_key, shape, width, bound, cuts=(), kind=jnp.bfloat16):
    result = jax.random.normal(own_key, shape, jnp.float32) * width
    if len(cuts) > 0:
        result = shard_levels(own_key, shape, cuts, -0.22, 0.18) * result
    return jnp.clip(result, min=-bound, max=bound).astype(kind)


def setup_inputs(seed: int = 0) -> dict:
    splits = jax.random.split(jax.random.key(seed), 9)
    return {
        "sketch": gaussian(splits[0], (SAMPLES, ORDER), 1.0, 6.0, ((0, 8), (1, 64)), jnp.float32),
        "probes": gaussian(splits[1], (SAMPLES, ORDER), 1.0, 6.0, ((0, 8), (1, 64)), jnp.float32),
        "test_leaf": gaussian(splits[2], (RANK, SAMPLES), SAMPLES ** -0.5, 0.375, (), jnp.float32),
        "test_parent": gaussian(splits[3], (RANK, SAMPLES), SAMPLES ** -0.5, 0.375, (), jnp.float32),
        "leaf_far": draw_leaf_far(jax.random.fold_in(splits[8], 71), 0),
        "leaf_count": draw_leaf_count(jax.random.fold_in(splits[8], 71), 0),
        "parent_far": draw_parent_far(jax.random.fold_in(splits[8], 71), 0),
        "parent_count": draw_parent_count(jax.random.fold_in(splits[8], 71), 0),
    }


highest = lax.Precision.HIGHEST

def orthonormal(blocks):
    gram_matrix = jnp.einsum('nrl,ntl->nrt', blocks, blocks, precision=highest)
    factor = jnp.linalg.cholesky(gram_matrix)
    return jax.scipy.linalg.solve_triangular(factor, blocks, lower=True)

def reference(sketch, probes, test_leaf, test_parent, leaf_far, leaf_count, parent_far, parent_count):
    sketch_cols = sketch.reshape(SAMPLES, LEAVES, LEAF)
    probe_cols = probes.reshape(SAMPLES, LEAVES, LEAF)
    blocks = jnp.einsum('rs,sil->irl', test_leaf, sketch_cols, precision=highest)
    orthobasis = orthonormal(blocks)
    leaf_basis = orthobasis.transpose(1, 0, 2).reshape(RANK, ORDER)
    wproj = jnp.einsum('irl,sil->sir', orthobasis, sketch_cols, precision=highest)
    vproj = jnp.einsum('irl,sil->sir', orthobasis, probe_cols, precision=highest)
    slot_ids = jnp.arange(NFAR, dtype=jnp.int32)
    leaf_mask = (slot_ids[None, :] < leaf_count[:, None]).astype(jnp.float32)
    leaf_terms = []
    for position in range(NFAR):
        partner = vproj[:, leaf_far[:, position], :]
        leaf_terms.append(jnp.einsum('sir,sit->irt', wproj, partner, precision=highest))
    leaf_coupling = jnp.stack(leaf_terms, axis=1) * leaf_mask[:, :, None, None] / SAMPLES
    leaf_coupling = leaf_coupling.reshape(LEAVES, NFAR, RANK * RANK)
    stacked = wproj.reshape(SAMPLES, PARENTS, 2 * RANK)
    vstacked = vproj.reshape(SAMPLES, PARENTS, 2 * RANK)
    parent_blocks = jnp.einsum('rs,spc->prc', test_parent, stacked, precision=highest)
    transfer = orthonormal(parent_blocks)
    wcoarse = jnp.einsum('prc,spc->spr', transfer, stacked, precision=highest).astype(jnp.bfloat16)
    vcoarse = jnp.einsum('prc,spc->spr', transfer, vstacked, precision=highest).astype(jnp.bfloat16)
    parent_mask = (slot_ids[None, :] < parent_count[:, None]).astype(jnp.float32)
    parent_terms = []
    for position in range(NFAR):
        partner = vcoarse[:, parent_far[:, position], :].astype(jnp.float32)
        parent_terms.append(jnp.einsum('spr,spt->prt', wcoarse.astype(jnp.float32), partner, precision=highest))
    parent_coupling = jnp.stack(parent_terms, axis=1) * parent_mask[:, :, None, None] / SAMPLES
    parent_coupling = parent_coupling.reshape(PARENTS, NFAR, RANK * RANK)
    return (leaf_basis, leaf_coupling, transfer, parent_coupling)
```

```python
import functools
import jax
import jax.numpy as jnp
from jax import lax
from jax.experimental import pallas as pl
from jax.experimental.pallas import tpu as pltpu
from jax.sharding import PartitionSpec as P

f32 = jnp.float32
bf16 = jnp.bfloat16

LEAF = 256
RANK = 64
REACH = 4
SCALE = 8192.0


def split(x):
    high = x.astype(bf16)
    low = (x - high.astype(f32)).astype(bf16)
    return high, low


def product(a, b, contract):
    dims = ((contract[0],), (contract[1],)), ((), ())
    dot = functools.partial(lax.dot_general, dimension_numbers=dims, preferred_element_type=f32)
    return dot(a[0], b[0]) + (dot(a[1], b[0]) + dot(a[0], b[1]))


def inverse_factors(packs):
    tiles = RANK // 8
    lane = lax.broadcasted_iota(jnp.int32, (8, 128), 1)
    sub = lax.broadcasted_iota(jnp.int32, (8, 128), 0)
    column = lane % RANK
    half = lane - column

    def row(x, k):
        return jnp.broadcast_to(x[k : k + 1, :], (8, 128))

    state = [[p[8 * t : 8 * t + 8, :] for t in range(tiles)] for p in packs]
    for block in range(tiles):
        start = 8 * block
        cols = [
            [
                [jnp.take_along_axis(s[t], half + (start + k), axis=1) for t in range(block, tiles)]
                for k in range(8)
            ]
            for s in state
        ]
        inside = (column >= start) & (column < start + 8)
        unit = jnp.where(column == start + sub, 1.0, 0.0).astype(f32)
        for s, c in zip(state, cols):
            head = jnp.where(inside, unit, s[block])
            rest = [jnp.where(inside, 0.0, s[t]) for t in range(block + 1, tiles)]
            pivots = jnp.ones((8, 128), f32)
            for k in range(8):
                pivot = row(c[k][0], k)
                pivots = jnp.where(sub == k, pivot, pivots)
                inv = 1.0 / pivot
                mult = [x * inv for x in c[k]]
                mult[0] = jnp.where(sub > k, mult[0], 0.0)
                for k2 in range(k + 1, 8):
                    factor = row(c[k][0], k2)
                    c[k2] = [x - m * factor for x, m in zip(c[k2], mult)]
                lead = row(head, k)
                head = head - mult[0] * lead
                rest = [x - m * lead for x, m in zip(rest, mult[1:])]
            head = head * lax.rsqrt(pivots)
            s[block] = jnp.where(column <= start + sub, head, 0.0)
            s[block + 1 :] = rest
    return [jnp.concatenate(s, axis=0) for s in state]


def inverses(grams):
    padded = list(grams) + ([grams[-1]] if len(grams) % 2 else [])
    packs = [jnp.concatenate(padded[i : i + 2], axis=1) for i in range(0, len(padded), 2)]
    done = inverse_factors(packs)
    out = []
    for p in done:
        out += [p[:, :RANK], p[:, RANK:]]
    return out[: len(grams)]


def keep(halves, i, value):
    for h, half in enumerate(halves):
        half[RANK * i : RANK * i + RANK, :] = value[:, 128 * h : 128 * h + 128]


def deinterleave(halves, i, out_ref):
    for h, half in enumerate(halves):
        for odd in range(2):
            rows = half[pl.ds(RANK * i + odd, RANK // 2, stride=2), :]
            start = RANK * i + RANK // 2 * odd
            out_ref[start : start + RANK // 2, 128 * h : 128 * h + 128] = rows.astype(bf16)


def compress(y_ref, test_ref, ptest_ref, basis_ref, w_ref, transfer_ref, a_ref, *halves):
    owned = y_ref.shape[1] // LEAF
    parents = owned // 2
    test = split(test_ref[...])
    ys, ks, grams = [], [], []
    for i in range(owned):
        y = split(y_ref[:, LEAF * i : LEAF * i + LEAF])
        ys.append(y)
        k = split(product(test, y, (1, 0)))
        ks.append(k)
        grams.append(product(k, k, (1, 1)))
    linvs = inverses(grams)
    ptest = split(ptest_ref[...])
    for i in range(owned):
        q = product(split(linvs[i]), ks[i], (1, 0))
        basis_ref[:, LEAF * i : LEAF * i + LEAF] = q
        keep(halves, i, product(split(q), ys[i], (1, 1)))
    blocks, stacks, grams = [], [], []
    for p in range(parents):
        stack = [h[2 * RANK * p : 2 * RANK * (p + 1), :] for h in halves]
        stack = split(jnp.concatenate(stack, axis=1))
        stacks.append(stack)
        c = split(product(ptest, stack, (1, 1)))
        blocks.append(c)
        grams.append(product(c, c, (1, 1)))
    for i in range(owned):
        deinterleave(halves, i, w_ref)
    finvs = inverses(grams)
    for p in range(parents):
        x = product(split(finvs[p]), blocks[p], (1, 0))
        transfer_ref[p] = x
        keep(halves, p, product(split(x), stacks[p], (1, 0)))
        deinterleave(halves, p, a_ref)


def project(o_ref, basis_ref, transfer_ref, v_ref, b_ref):
    owned = o_ref.shape[1] // LEAF
    for p in range(owned // 2):
        pair = []
        for i in (2 * p, 2 * p + 1):
            q = split(basis_ref[:, LEAF * i : LEAF * i + LEAF])
            v = product(q, split(o_ref[:, LEAF * i : LEAF * i + LEAF]), (1, 1))
            v_ref[RANK * i : RANK * i + RANK, :] = v.astype(bf16)
            pair.append(v)
        stack = split(jnp.concatenate(pair, axis=0))
        b_ref[RANK * p : RANK * p + RANK, :] = product(split(transfer_ref[p]), stack, (1, 0)).astype(bf16)


def couple(far_ref, count_ref, left_ref, *refs):
    pieces, out_ref, table = refs[:-2], refs[-2], refs[-1]
    rows = left_ref.shape[0] // RANK
    slots = far_ref.shape[1]
    at = 0
    for piece in pieces:
        size = piece.shape[0] // RANK
        for j in range(size):
            table[at + j] = piece[RANK * j : RANK * j + RANK, :]
        at += size
    lane = lax.broadcasted_iota(jnp.int32, (RANK // 2, 128), 1)
    low = lane < RANK
    samples = left_ref.shape[1]
    dims = (((1,), (1,)), ((), ()))
    for i in range(rows):
        left = left_ref[RANK * i : RANK * i + RANK, :]
        for k in range(0, slots, 2):
            right = jnp.concatenate([table[far_ref[i, k + e]] for e in range(2)], axis=0)
            x = lax.dot_general(left, right, dims, preferred_element_type=f32)
            even, odd = x[: RANK // 2], x[RANK // 2 :]
            first = jnp.where(low, even, pltpu.roll(odd, RANK, 1))
            second = jnp.where(low, pltpu.roll(even, RANK, 1), odd)
            for e, value in enumerate((first, second)):
                scale = jnp.where(k + e < count_ref[i], 1.0 / samples, 0.0).astype(f32)
                out_ref[pl.ds(i * 4 * RANK + k + e, RANK // 2, stride=8), :] = value * scale


vmem = pl.BlockSpec(memory_space=pltpu.VMEM)
smem = pl.BlockSpec(memory_space=pltpu.SMEM)


def run_compress(y, test, ptest):
    owned = y.shape[1] // LEAF
    samples = y.shape[0]
    return pl.pallas_call(
        compress,
        out_shape=(
            jax.ShapeDtypeStruct((RANK, y.shape[1]), f32),
            jax.ShapeDtypeStruct((owned * RANK, samples), bf16),
            jax.ShapeDtypeStruct((owned // 2, RANK, 2 * RANK), f32),
            jax.ShapeDtypeStruct((owned // 2 * RANK, samples), bf16),
        ),
        in_specs=[vmem] * 3,
        out_specs=(vmem,) * 4,
        scratch_shapes=[pltpu.VMEM((owned * RANK, 128), f32)] * (samples // 128),
        name="compress",
    )(y, test, ptest)


def run_project(o, basis, transfer):
    owned = o.shape[1] // LEAF
    samples = o.shape[0]
    return pl.pallas_call(
        project,
        out_shape=(
            jax.ShapeDtypeStruct((owned * RANK, samples), bf16),
            jax.ShapeDtypeStruct((owned // 2 * RANK, samples), bf16),
        ),
        in_specs=[vmem] * 3,
        out_specs=(vmem,) * 2,
        name="project",
    )(o, basis, transfer)


def run_couple(far, count, left, pieces, name):
    rows, slots = far.shape
    total = sum(p.shape[0] for p in pieces) // RANK
    out = pl.pallas_call(
        couple,
        out_shape=jax.ShapeDtypeStruct((rows * 4 * RANK, 128), f32),
        in_specs=[smem, smem, vmem] + [vmem] * len(pieces),
        out_specs=vmem,
        scratch_shapes=[pltpu.VMEM((total, RANK, left.shape[1]), bf16)],
        name=name,
    )(far, count, left, *pieces)
    out = out.reshape(rows, RANK // 2, slots, 128)
    return out.transpose(0, 2, 1, 3).reshape(rows, slots, RANK * RANK)


def gathered(array):
    devices = lax.axis_size("samp")
    rows, columns = array.shape
    sent = (array * SCALE).astype(jnp.float16).reshape(rows, devices, columns // devices).transpose(1, 0, 2)
    got = lax.all_to_all(sent, "samp", split_axis=0, concat_axis=0, tiled=True)
    return got.astype(f32).reshape(rows * devices, columns // devices) * (1.0 / SCALE)


def shifted(array, axis, by):
    devices = lax.axis_size(axis)
    pairs = [(i, (i - by) % devices) for i in range(devices)]
    return lax.ppermute(array, axis, pairs)


def body(sketch, probes, test_leaf, test_parent, leaf_far, leaf_count, parent_far, parent_count):
    owned = leaf_far.shape[0]
    per_device = parent_far.shape[0]
    y = gathered(sketch)
    o = gathered(probes)
    basis, w, transfer, a = run_compress(y, test_leaf, test_parent)
    v, b = run_project(o, basis, transfer)
    before, after = shifted(b, "rows", -1), shifted(b, "rows", 1)
    near = jnp.concatenate([before, b, after], axis=0)
    v_before, v_after = shifted(v, ("rows", "samp"), -1), shifted(v, ("rows", "samp"), 1)
    far_before, far_after = shifted(near, "rows", -3), shifted(near, "rows", 3)
    first_leaf = lax.axis_index(("rows", "samp")) * owned
    leaf_at = jnp.clip(leaf_far - first_leaf + owned, 0, 3 * owned - 1)
    leaf_coupling = run_couple(leaf_at, leaf_count, w, [v_before, v, v_after], "leaf")
    row = parent_far // (per_device * lax.axis_size("samp"))
    step = row - lax.axis_index("rows") + REACH
    parent_at = jnp.clip(step * per_device + parent_far % per_device, 0, (2 * REACH + 1) * per_device - 1)
    parent_coupling = run_couple(parent_at, parent_count, a, [far_before, near, far_after], "parent")
    return (basis, leaf_coupling, transfer, parent_coupling)


def solution(mesh):
    return jax.shard_map(
        body,
        mesh=mesh,
        in_specs=(
            P("samp", "rows"),
            P("samp", "rows"),
            P(),
            P(),
            P(("rows", "samp"), None),
            P(("rows", "samp")),
            P(("rows", "samp"), None),
            P(("rows", "samp")),
        ),
        out_specs=(
            P(None, ("rows", "samp")),
            P(("rows", "samp"), None, None),
            P(("rows", "samp"), None, None),
            P(("rows", "samp"), None, None),
        ),
        check_vma=False,
    )
```

```python
import functools
import jax
import jax.numpy as jnp
from jax import lax
from jax.experimental import pallas as pl
from jax.experimental.pallas import tpu as pltpu
from jax.sharding import PartitionSpec as P


f32 = jnp.float32
bf16 = jnp.bfloat16

LEAF = 256
RANK = 64
REACH = 4
SCALE = 8192.0


def split(x):
    high = x.astype(bf16)
    low = (x - high.astype(f32)).astype(bf16)
    return high, low


def product(a, b, contract):
    dims = ((contract[0],), (contract[1],)), ((), ())
    dot = functools.partial(lax.dot_general, dimension_numbers=dims, preferred_element_type=f32)
    return dot(a[0], b[0]) + (dot(a[1], b[0]) + dot(a[0], b[1]))


def inverse_factors(packs):
    tiles = RANK // 8
    lane = lax.broadcasted_iota(jnp.int32, (8, 128), 1)
    sub = lax.broadcasted_iota(jnp.int32, (8, 128), 0)
    column = lane % RANK
    half = lane - column

    def row(x, k):
        return jnp.broadcast_to(x[k : k + 1, :], (8, 128))

    state = [[p[8 * t : 8 * t + 8, :] for t in range(tiles)] for p in packs]
    for block in range(tiles):
        start = 8 * block
        cols = [
            [
                [jnp.take_along_axis(s[t], half + (start + k), axis=1) for t in range(block, tiles)]
                for k in range(8)
            ]
            for s in state
        ]
        inside = (column >= start) & (column < start + 8)
        unit = jnp.where(column == start + sub, 1.0, 0.0).astype(f32)
        for s, c in zip(state, cols):
            head = jnp.where(inside, unit, s[block])
            rest = [jnp.where(inside, 0.0, s[t]) for t in range(block + 1, tiles)]
            pivots = jnp.ones((8, 128), f32)
            for k in range(8):
                pivot = row(c[k][0], k)
                pivots = jnp.where(sub == k, pivot, pivots)
                inv = 1.0 / pivot
                mult = [x * inv for x in c[k]]
                mult[0] = jnp.where(sub > k, mult[0], 0.0)
                for k2 in range(k + 1, 8):
                    factor = row(c[k][0], k2)
                    c[k2] = [x - m * factor for x, m in zip(c[k2], mult)]
                lead = row(head, k)
                head = head - mult[0] * lead
                rest = [x - m * lead for x, m in zip(rest, mult[1:])]
            head = head * lax.rsqrt(pivots)
            s[block] = jnp.where(column <= start + sub, head, 0.0)
            s[block + 1 :] = rest
    return [jnp.concatenate(s, axis=0) for s in state]


def inverses(grams):
    padded = list(grams) + ([grams[-1]] if len(grams) % 2 else [])
    packs = [jnp.concatenate(padded[i : i + 2], axis=1) for i in range(0, len(padded), 2)]
    done = inverse_factors(packs)
    out = []
    for p in done:
        out += [p[:, :RANK], p[:, RANK:]]
    return out[: len(grams)]


def keep(halves, i, value):
    for h, half in enumerate(halves):
        half[RANK * i : RANK * i + RANK, :] = value[:, 128 * h : 128 * h + 128]


def deinterleave(halves, i, out_ref):
    for h, half in enumerate(halves):
        for odd in range(2):
            rows = half[pl.ds(RANK * i + odd, RANK // 2, stride=2), :]
            start = RANK * i + RANK // 2 * odd
            out_ref[start : start + RANK // 2, 128 * h : 128 * h + 128] = rows.astype(bf16)


def compress(y_ref, test_ref, ptest_ref, basis_ref, w_ref, transfer_ref, a_ref, *halves):
    owned = y_ref.shape[1] // LEAF
    parents = owned // 2
    test = split(test_ref[...])
    ys, ks, grams = [], [], []
    for i in range(owned):
        y = split(y_ref[:, LEAF * i : LEAF * i + LEAF])
        ys.append(y)
        k = split(product(test, y, (1, 0)))
        ks.append(k)
        grams.append(product(k, k, (1, 1)))
    linvs = inverses(grams)
    ptest = split(ptest_ref[...])
    for i in range(owned):
        q = product(split(linvs[i]), ks[i], (1, 0))
        basis_ref[:, LEAF * i : LEAF * i + LEAF] = q
        keep(halves, i, product(split(q), ys[i], (1, 1)))
    blocks, stacks, grams = [], [], []
    for p in range(parents):
        stack = [h[2 * RANK * p : 2 * RANK * (p + 1), :] for h in halves]
        stack = split(jnp.concatenate(stack, axis=1))
        stacks.append(stack)
        c = split(product(ptest, stack, (1, 1)))
        blocks.append(c)
        grams.append(product(c, c, (1, 1)))
    for i in range(owned):
        deinterleave(halves, i, w_ref)
    finvs = inverses(grams)
    for p in range(parents):
        x = product(split(finvs[p]), blocks[p], (1, 0))
        transfer_ref[p] = x
        keep(halves, p, product(split(x), stacks[p], (1, 0)))
        deinterleave(halves, p, a_ref)


def project(o_ref, basis_ref, transfer_ref, v_ref, b_ref):
    owned = o_ref.shape[1] // LEAF
    for p in range(owned // 2):
        pair = []
        for i in (2 * p, 2 * p + 1):
            q = split(basis_ref[:, LEAF * i : LEAF * i + LEAF])
            v = product(q, split(o_ref[:, LEAF * i : LEAF * i + LEAF]), (1, 1))
            v_ref[RANK * i : RANK * i + RANK, :] = v.astype(bf16)
            pair.append(v)
        stack = split(jnp.concatenate(pair, axis=0))
        b_ref[RANK * p : RANK * p + RANK, :] = product(split(transfer_ref[p]), stack, (1, 0)).astype(bf16)


def couple(place, far_ref, count_ref, left_ref, *refs):
    pieces, out_ref, table = refs[:-2], refs[-2], refs[-1]
    rows = left_ref.shape[0] // RANK
    slots = far_ref.shape[1]
    at = 0
    for piece in pieces:
        size = piece.shape[0] // RANK
        for j in range(size):
            table[at + j] = piece[RANK * j : RANK * j + RANK, :]
        at += size
    lane = lax.broadcasted_iota(jnp.int32, (RANK // 2, 128), 1)
    low = lane < RANK
    samples = left_ref.shape[1]
    dims = (((1,), (1,)), ((), ()))
    spot = place()
    for i in range(rows):
        left = left_ref[RANK * i : RANK * i + RANK, :]
        for k in range(0, slots, 2):
            right = jnp.concatenate([table[jnp.clip(spot(far_ref[i, k + e]), 0, at - 1)] for e in range(2)], axis=0)
            x = lax.dot_general(left, right, dims, preferred_element_type=f32)
            even, odd = x[: RANK // 2], x[RANK // 2 :]
            first = jnp.where(low, even, pltpu.roll(odd, RANK, 1))
            second = jnp.where(low, pltpu.roll(even, RANK, 1), odd)
            for e, value in enumerate((first, second)):
                scale = jnp.where(k + e < count_ref[i], 1.0 / samples, 0.0).astype(f32)
                out_ref[pl.ds(i * 4 * RANK + k + e, RANK // 2, stride=8), :] = value * scale


vmem = pl.BlockSpec(memory_space=pltpu.VMEM)
smem = pl.BlockSpec(memory_space=pltpu.SMEM)
params = pltpu.CompilerParams(vmem_limit_bytes=16 << 20)


def cost(us):
    return pl.CostEstimate(flops=us * 10**9, bytes_accessed=us * 10**6, transcendentals=0)


def run_compress(y, test, ptest):
    owned = y.shape[1] // LEAF
    samples = y.shape[0]
    return pl.pallas_call(
        compress,
        out_shape=(
            jax.ShapeDtypeStruct((RANK, y.shape[1]), f32),
            jax.ShapeDtypeStruct((owned * RANK, samples), bf16),
            jax.ShapeDtypeStruct((owned // 2, RANK, 2 * RANK), f32),
            jax.ShapeDtypeStruct((owned // 2 * RANK, samples), bf16),
        ),
        in_specs=[vmem] * 3,
        out_specs=(vmem,) * 4,
        scratch_shapes=[pltpu.VMEM((owned * RANK, 128), f32)] * (samples // 128),
        compiler_params=params,
        cost_estimate=cost(12),
        name="compress",
    )(y, test, ptest)


def run_project(o, basis, transfer):
    owned = o.shape[1] // LEAF
    samples = o.shape[0]
    return pl.pallas_call(
        project,
        out_shape=(
            jax.ShapeDtypeStruct((owned * RANK, samples), bf16),
            jax.ShapeDtypeStruct((owned // 2 * RANK, samples), bf16),
        ),
        in_specs=[vmem] * 3,
        out_specs=(vmem,) * 2,
        compiler_params=params,
        cost_estimate=cost(4),
        name="project",
    )(o, basis, transfer)


def run_couple(place, far, count, left, pieces):
    rows, slots = far.shape
    total = sum(p.shape[0] for p in pieces) // RANK
    out = pl.pallas_call(
        functools.partial(couple, place),
        out_shape=jax.ShapeDtypeStruct((rows * 4 * RANK, 128), f32),
        in_specs=[smem, smem, vmem] + [vmem] * len(pieces),
        out_specs=vmem,
        scratch_shapes=[pltpu.VMEM((total, RANK, left.shape[1]), bf16)],
        compiler_params=params,
        cost_estimate=cost(3),
    )(far, count, left, *pieces)
    out = out.reshape(rows, RANK // 2, slots, 128)
    return out.transpose(0, 2, 1, 3).reshape(rows, slots, RANK * RANK)


def gathered(array):
    devices = lax.axis_size("samp")
    rows, columns = array.shape
    sent = (array * SCALE).astype(jnp.float16).reshape(rows, devices, columns // devices).transpose(1, 0, 2)
    got = lax.all_to_all(sent, "samp", split_axis=0, concat_axis=0, tiled=True)
    return got.astype(f32).reshape(rows * devices, columns // devices) * (1.0 / SCALE)


def neighbours(size):
    up = [(i, i + 1) for i in range(size - 1)]
    return up, [(j, i) for i, j in up]


def far_pairs(rows):
    first, second = [], []
    for start in range(3):
        chain = list(range(start, rows, 3))
        for at, (i, j) in enumerate(zip(chain, chain[1:])):
            if start == 0:
                first.append((i, j))
                second.append((j, i))
            else:
                (second if at % 2 else first).extend([(i, j), (j, i)])
    second.append((0, 2))
    first.append((rows - 1, rows - 3))
    got = [[{r}, {r}] for r in range(rows)]
    for pairs in (first, second):
        assert len({i for i, _ in pairs}) == len({j for _, j in pairs}) == len(pairs)
        for i, j in pairs:
            got[j][1] |= {i - 1, i, i + 1}
    for r in range(rows):
        have = got[r][1] | {r - 1, r + 1}
        assert all(q in have for q in range(max(r - REACH, 0), min(r + REACH + 1, rows)))
    return first, second


def body(sketch, probes, test_leaf, test_parent, leaf_far, leaf_count, parent_far, parent_count):
    owned = leaf_far.shape[0]
    per_device = parent_far.shape[0]
    row_count = lax.axis_size("rows")
    samp_count = lax.axis_size("samp")
    y = gathered(sketch)
    o = gathered(probes)
    basis, w, transfer, a = run_compress(y, test_leaf, test_parent)
    v, b = run_project(o, basis, transfer)
    up, down = neighbours(row_count)
    near = [lax.ppermute(b, "rows", up), b, lax.ppermute(b, "rows", down)]
    near = jnp.concatenate(near, axis=0)
    both = ("rows", "samp")
    up, down = neighbours(lax.axis_size(both))
    halo = [lax.ppermute(v, both, up), v, lax.ppermute(v, both, down)]
    pairs = far_pairs(row_count)
    far = [lax.ppermute(near, "rows", pairs[e]) for e in range(2)]

    def leaf_place():
        before = lax.axis_index(both) * owned - owned
        return lambda leaf: leaf - before

    def parent_place():
        row = lax.axis_index("rows")
        ahead = lax.rem(row, 6)
        one = jnp.where((ahead == 0) | (ahead == 3) | (ahead == 4) | (ahead == 5), -REACH + 1, REACH - 1)
        one = jnp.where(row == row_count - 3, 2, one)
        two = jnp.where((ahead == 1) | (ahead == 2), -REACH + 1, REACH - 1)
        two = jnp.where(row == 2, -2, two)
        across = per_device * samp_count

        def spot(parent):
            away = lax.div(parent, across) - row
            far_at = jnp.where(abs(away - one) <= 1, away - one + 4, away - two + 7)
            at = jnp.where(abs(away) <= 1, away + 1, far_at)
            return at * per_device + lax.rem(parent, per_device)

        return spot

    leaf_coupling = run_couple(leaf_place, leaf_far, leaf_count, w, halo)
    parent_coupling = run_couple(parent_place, parent_far, parent_count, a, [near, *far])
    return (basis, leaf_coupling, transfer, parent_coupling)


def solution(mesh):
    return jax.shard_map(
        body,
        mesh=mesh,
        in_specs=(
            P("samp", "rows"),
            P("samp", "rows"),
            P(),
            P(),
            P(("rows", "samp"), None),
            P(("rows", "samp")),
            P(("rows", "samp"), None),
            P(("rows", "samp")),
        ),
        out_specs=(
            P(None, ("rows", "samp")),
            P(("rows", "samp"), None, None),
            P(("rows", "samp"), None, None),
            P(("rows", "samp"), None, None),
        ),
        check_vma=False,
    )
```

```python
import functools
import jax
import jax.numpy as jnp
from jax import lax
from jax.experimental import pallas as pl
from jax.experimental.pallas import tpu as pltpu
from jax.sharding import PartitionSpec as P


f32 = jnp.float32
bf16 = jnp.bfloat16

LEAF = 256
RANK = 64
REACH = 4
SCALE = 8192.0


def split(x):
    high = x.astype(bf16)
    low = (x - high.astype(f32)).astype(bf16)
    return high, low


def product(a, b, contract):
    dims = ((contract[0],), (contract[1],)), ((), ())
    dot = functools.partial(lax.dot_general, dimension_numbers=dims, preferred_element_type=f32)
    return dot(a[0], b[0]) + (dot(a[1], b[0]) + dot(a[0], b[1]))


def inverse_factors(packs):
    tiles = RANK // 8
    lane = lax.broadcasted_iota(jnp.int32, (8, 128), 1)
    sub = lax.broadcasted_iota(jnp.int32, (8, 128), 0)
    column = lane % RANK
    half = lane - column

    def row(x, k):
        return jnp.broadcast_to(x[k : k + 1, :], (8, 128))

    state = [[p[8 * t : 8 * t + 8, :] for t in range(tiles)] for p in packs]
    for block in range(tiles):
        start = 8 * block
        cols = [
            [
                [jnp.take_along_axis(s[t], half + (start + k), axis=1) for t in range(block, tiles)]
                for k in range(8)
            ]
            for s in state
        ]
        inside = (column >= start) & (column < start + 8)
        unit = jnp.where(column == start + sub, 1.0, 0.0).astype(f32)
        for s, c in zip(state, cols):
            head = jnp.where(inside, unit, s[block])
            rest = [jnp.where(inside, 0.0, s[t]) for t in range(block + 1, tiles)]
            pivots = jnp.ones((8, 128), f32)
            for k in range(8):
                pivot = row(c[k][0], k)
                pivots = jnp.where(sub == k, pivot, pivots)
                inv = 1.0 / pivot
                mult = [x * inv for x in c[k]]
                mult[0] = jnp.where(sub > k, mult[0], 0.0)
                for k2 in range(k + 1, 8):
                    factor = row(c[k][0], k2)
                    c[k2] = [x - m * factor for x, m in zip(c[k2], mult)]
                lead = row(head, k)
                head = head - mult[0] * lead
                rest = [x - m * lead for x, m in zip(rest, mult[1:])]
            head = head * lax.rsqrt(pivots)
            s[block] = jnp.where(column <= start + sub, head, 0.0)
            s[block + 1 :] = rest
    return [jnp.concatenate(s, axis=0) for s in state]


def inverses(grams):
    padded = list(grams) + ([grams[-1]] if len(grams) % 2 else [])
    packs = [jnp.concatenate(padded[i : i + 2], axis=1) for i in range(0, len(padded), 2)]
    done = inverse_factors(packs)
    out = []
    for p in done:
        out += [p[:, :RANK], p[:, RANK:]]
    return out[: len(grams)]


def keep(halves, i, value):
    for h, half in enumerate(halves):
        half[RANK * i : RANK * i + RANK, :] = value[:, 128 * h : 128 * h + 128]


def deinterleave(halves, i, out_ref):
    for h, half in enumerate(halves):
        for odd in range(2):
            rows = half[pl.ds(RANK * i + odd, RANK // 2, stride=2), :]
            start = RANK * i + RANK // 2 * odd
            out_ref[start : start + RANK // 2, 128 * h : 128 * h + 128] = rows.astype(bf16)


def compress(y_ref, test_ref, ptest_ref, basis_ref, w_ref, transfer_ref, a_ref, *halves):
    owned = y_ref.shape[1] // LEAF
    parents = owned // 2
    test = split(test_ref[...])
    ys, ks, grams = [], [], []
    for i in range(owned):
        y = split(y_ref[:, LEAF * i : LEAF * i + LEAF])
        ys.append(y)
        k = split(product(test, y, (1, 0)))
        ks.append(k)
        grams.append(product(k, k, (1, 1)))
    linvs = inverses(grams)
    ptest = split(ptest_ref[...])
    for i in range(owned):
        q = product(split(linvs[i]), ks[i], (1, 0))
        basis_ref[:, LEAF * i : LEAF * i + LEAF] = q
        keep(halves, i, product(split(q), ys[i], (1, 1)))
    blocks, stacks, grams = [], [], []
    for p in range(parents):
        stack = [h[2 * RANK * p : 2 * RANK * (p + 1), :] for h in halves]
        stack = split(jnp.concatenate(stack, axis=1))
        stacks.append(stack)
        c = split(product(ptest, stack, (1, 1)))
        blocks.append(c)
        grams.append(product(c, c, (1, 1)))
    for i in range(owned):
        deinterleave(halves, i, w_ref)
    finvs = inverses(grams)
    for p in range(parents):
        x = product(split(finvs[p]), blocks[p], (1, 0))
        transfer_ref[p] = x
        keep(halves, p, product(split(x), stacks[p], (1, 0)))
        deinterleave(halves, p, a_ref)


def project(o_ref, basis_ref, transfer_ref, v_ref, b_ref):
    owned = o_ref.shape[1] // LEAF
    for p in range(owned // 2):
        pair = []
        for i in (2 * p, 2 * p + 1):
            q = split(basis_ref[:, LEAF * i : LEAF * i + LEAF])
            v = product(q, split(o_ref[:, LEAF * i : LEAF * i + LEAF]), (1, 1))
            v_ref[RANK * i : RANK * i + RANK, :] = v.astype(bf16)
            pair.append(v)
        stack = split(jnp.concatenate(pair, axis=0))
        b_ref[RANK * p : RANK * p + RANK, :] = product(split(transfer_ref[p]), stack, (1, 0)).astype(bf16)


def couple(place, far_ref, count_ref, left_ref, *refs):
    pieces, out_ref, table = refs[:-2], refs[-2], refs[-1]
    rows = left_ref.shape[0] // RANK
    slots = far_ref.shape[1]
    at = 0
    for piece in pieces:
        size = piece.shape[0] // RANK
        for j in range(size):
            table[at + j] = piece[RANK * j : RANK * j + RANK, :]
        at += size
    lane = lax.broadcasted_iota(jnp.int32, (RANK // 2, 128), 1)
    low = lane < RANK
    samples = left_ref.shape[1]
    dims = (((1,), (1,)), ((), ()))
    spot = place()
    for i in range(rows):
        left = left_ref[RANK * i : RANK * i + RANK, :]
        for k in range(0, slots, 2):
            right = jnp.concatenate([table[jnp.clip(spot(far_ref[i, k + e]), 0, at - 1)] for e in range(2)], axis=0)
            x = lax.dot_general(left, right, dims, preferred_element_type=f32)
            even, odd = x[: RANK // 2], x[RANK // 2 :]
            first = jnp.where(low, even, pltpu.roll(odd, RANK, 1))
            second = jnp.where(low, pltpu.roll(even, RANK, 1), odd)
            for e, value in enumerate((first, second)):
                scale = jnp.where(k + e < count_ref[i], 1.0 / samples, 0.0).astype(f32)
                out_ref[pl.ds(i * 4 * RANK + k + e, RANK // 2, stride=8), :] = value * scale


vmem = pl.BlockSpec(memory_space=pltpu.VMEM)
smem = pl.BlockSpec(memory_space=pltpu.SMEM)
params = pltpu.CompilerParams(vmem_limit_bytes=16 << 20)


def cost(us):
    return pl.CostEstimate(flops=us * 10**9, bytes_accessed=us * 10**6, transcendentals=0)


def run_compress(y, test, ptest):
    owned = y.shape[1] // LEAF
    samples = y.shape[0]
    return pl.pallas_call(
        compress,
        out_shape=(
            jax.ShapeDtypeStruct((RANK, y.shape[1]), f32),
            jax.ShapeDtypeStruct((owned * RANK, samples), bf16),
            jax.ShapeDtypeStruct((owned // 2, RANK, 2 * RANK), f32),
            jax.ShapeDtypeStruct((owned // 2 * RANK, samples), bf16),
        ),
        in_specs=[vmem] * 3,
        out_specs=(vmem,) * 4,
        scratch_shapes=[pltpu.VMEM((owned * RANK, 128), f32)] * (samples // 128),
        compiler_params=params,
        cost_estimate=cost(12),
        name="compress",
    )(y, test, ptest)


def run_project(o, basis, transfer):
    owned = o.shape[1] // LEAF
    samples = o.shape[0]
    return pl.pallas_call(
        project,
        out_shape=(
            jax.ShapeDtypeStruct((owned * RANK, samples), bf16),
            jax.ShapeDtypeStruct((owned // 2 * RANK, samples), bf16),
        ),
        in_specs=[vmem] * 3,
        out_specs=(vmem,) * 2,
        compiler_params=params,
        cost_estimate=cost(4),
        name="project",
    )(o, basis, transfer)


def run_couple(place, far, count, left, pieces):
    rows, slots = far.shape
    total = sum(p.shape[0] for p in pieces) // RANK
    out = pl.pallas_call(
        functools.partial(couple, place),
        out_shape=jax.ShapeDtypeStruct((rows * 4 * RANK, 128), f32),
        in_specs=[smem, smem, vmem] + [vmem] * len(pieces),
        out_specs=vmem,
        scratch_shapes=[pltpu.VMEM((total, RANK, left.shape[1]), bf16)],
        compiler_params=params,
        cost_estimate=cost(3),
    )(far, count, left, *pieces)
    out = out.reshape(rows, RANK // 2, slots, 128)
    return out.transpose(0, 2, 1, 3).reshape(rows, slots, RANK * RANK)


def gathered(array):
    devices = lax.axis_size("samp")
    rows, columns = array.shape
    sent = (array * SCALE).astype(jnp.float16).reshape(rows, devices, columns // devices).transpose(1, 0, 2)
    got = lax.all_to_all(sent, "samp", split_axis=0, concat_axis=0, tiled=True)
    return got.astype(f32).reshape(rows * devices, columns // devices) * (1.0 / SCALE)


def swaps(chain, late):
    found = []
    for i, j in list(zip(chain, chain[1:]))[late::2]:
        found += [(i, j), (j, i)]
    return found


def near_pairs(size):
    return swaps(range(size), 0), swaps(range(size), 1)


def far_pairs(rows):
    sets = [[], []]
    for start in range(3):
        for late in range(2):
            sets[late ^ (start == 1)] += swaps(range(start, rows, 3), late)
    sets[1] += [(0, 2), (rows - 1, rows - 3)]
    got = [{r} for r in range(rows)]
    for pairs in sets:
        assert len({i for i, _ in pairs}) == len({j for _, j in pairs}) == len(pairs)
        for i, j in pairs:
            got[j] |= {i - 1, i, i + 1}
    for r in range(rows):
        have = got[r] | {r - 1, r + 1}
        assert all(q in have for q in range(max(r - REACH, 0), min(r + REACH + 1, rows)))
    return sets


def body(sketch, probes, test_leaf, test_parent, leaf_far, leaf_count, parent_far, parent_count):
    owned = leaf_far.shape[0]
    per_device = parent_far.shape[0]
    row_count = lax.axis_size("rows")
    samp_count = lax.axis_size("samp")
    y = gathered(sketch)
    o = gathered(probes)
    basis, w, transfer, a = run_compress(y, test_leaf, test_parent)
    v, b = run_project(o, basis, transfer)
    pairs = near_pairs(row_count)
    near = [b] + [lax.ppermute(b, "rows", pairs[e]) for e in range(2)]
    near = jnp.concatenate(near, axis=0)
    both = ("rows", "samp")
    pairs = near_pairs(row_count * samp_count)
    halo = [v] + [lax.ppermute(v, both, pairs[e]) for e in range(2)]
    pairs = far_pairs(row_count)
    far = [lax.ppermute(near, "rows", pairs[e]) for e in range(2)]

    def leaf_place():
        own = lax.axis_index(both)
        first = own * owned
        odd = lax.rem(own, 2)

        def spot(leaf):
            later = (leaf >= first + owned).astype(jnp.int32)
            earlier = (leaf < first).astype(jnp.int32)
            piece = later * (1 + odd) + earlier * (2 - odd)
            return leaf - first + (earlier - later + piece) * owned

        return spot

    def parent_place():
        row = lax.axis_index("rows")
        odd = lax.rem(row, 2)
        start = lax.rem(row, 3)
        behind = (lax.rem(lax.div(row, 3), 2) == 1) != (start == 1)
        one = jnp.where(behind, -(REACH - 1), REACH - 1)
        two = -one
        two = jnp.where(row == 2, -2, two)
        two = jnp.where(row == row_count - 3, 2, two)
        across = per_device * samp_count

        def spot(parent):
            away = lax.div(parent, across) - row

            def among(there, centre):
                odd_there = lax.rem(row + centre + 2 * REACH, 2)
                return jnp.where(there == 0, 0, jnp.where((there == 1) == (odd_there == 0), 1, 2))

            far_at = jnp.where(abs(away - one) <= 1, 3 + among(away - one, one), 6 + among(away - two, two))
            at = jnp.where(abs(away) <= 1, among(away, 0), far_at)
            return at * per_device + lax.rem(parent, per_device)

        return spot

    leaf_coupling = run_couple(leaf_place, leaf_far, leaf_count, w, halo)
    parent_coupling = run_couple(parent_place, parent_far, parent_count, a, [near, *far])
    return (basis, leaf_coupling, transfer, parent_coupling)


def solution(mesh):
    return jax.shard_map(
        body,
        mesh=mesh,
        in_specs=(
            P("samp", "rows"),
            P("samp", "rows"),
            P(),
            P(),
            P(("rows", "samp"), None),
            P(("rows", "samp")),
            P(("rows", "samp"), None),
            P(("rows", "samp")),
        ),
        out_specs=(
            P(None, ("rows", "samp")),
            P(("rows", "samp"), None, None),
            P(("rows", "samp"), None, None),
            P(("rows", "samp"), None, None),
        ),
        check_vma=False,
    )
```

```python
import functools
import jax
import jax.numpy as jnp
from jax import lax
from jax.experimental import pallas as pl
from jax.experimental.pallas import tpu as pltpu
from jax.sharding import PartitionSpec as P


f32 = jnp.float32
bf16 = jnp.bfloat16

LEAF = 256
RANK = 64
REACH = 4
SCALE = 8192.0


def split(x):
    high = x.astype(bf16)
    low = (x - high.astype(f32)).astype(bf16)
    return high, low


def product(a, b, contract):
    dims = ((contract[0],), (contract[1],)), ((), ())
    dot = functools.partial(lax.dot_general, dimension_numbers=dims, preferred_element_type=f32)
    rows = a[0].shape[0]
    both = dot(jnp.concatenate(a, axis=0), b[0])
    return both[:rows] + (both[rows:] + dot(a[0], b[1]))


def gram(a):
    both = jnp.concatenate(a, axis=0)
    rows = a[0].shape[0]
    dims = (((1,), (1,)), ((), ()))
    full = lax.dot_general(both, both, dims, preferred_element_type=f32)
    total = full[:rows] + full[rows:]
    return total[:, :rows] + total[:, rows:]


def inverse_factors(packs):
    tiles = RANK // 8
    lane = lax.broadcasted_iota(jnp.int32, (8, 128), 1)
    sub = lax.broadcasted_iota(jnp.int32, (8, 128), 0)
    column = lane % RANK
    half = lane - column

    def row(x, k):
        return jnp.broadcast_to(x[k : k + 1, :], (8, 128))

    state = [[p[8 * t : 8 * t + 8, :] for t in range(tiles)] for p in packs]
    for block in range(tiles):
        start = 8 * block
        cols = [
            [
                [jnp.take_along_axis(s[t], half + (start + k), axis=1) for t in range(block, tiles)]
                for k in range(8)
            ]
            for s in state
        ]
        inside = (column >= start) & (column < start + 8)
        unit = jnp.where(column == start + sub, 1.0, 0.0).astype(f32)
        for s, c in zip(state, cols):
            head = jnp.where(inside, unit, s[block])
            rest = [jnp.where(inside, 0.0, s[t]) for t in range(block + 1, tiles)]
            pivots = jnp.ones((8, 128), f32)
            for k in range(8):
                pivot = row(c[k][0], k)
                pivots = jnp.where(sub == k, pivot, pivots)
                inv = 1.0 / pivot
                mult = [x * inv for x in c[k]]
                mult[0] = jnp.where(sub > k, mult[0], 0.0)
                for k2 in range(k + 1, 8):
                    factor = row(c[k][0], k2)
                    c[k2] = [x - m * factor for x, m in zip(c[k2], mult)]
                lead = row(head, k)
                head = head - mult[0] * lead
                rest = [x - m * lead for x, m in zip(rest, mult[1:])]
            head = head * lax.rsqrt(pivots)
            s[block] = jnp.where(column <= start + sub, head, 0.0)
            s[block + 1 :] = rest
    return [jnp.concatenate(s, axis=0) for s in state]


def inverses(grams):
    padded = list(grams) + ([grams[-1]] if len(grams) % 2 else [])
    packs = [jnp.concatenate(padded[i : i + 2], axis=1) for i in range(0, len(padded), 2)]
    done = inverse_factors(packs)
    out = []
    for p in done:
        out += [p[:, :RANK], p[:, RANK:]]
    return out[: len(grams)]


def keep(halves, i, value):
    for h, half in enumerate(halves):
        half[RANK * i : RANK * i + RANK, :] = value[:, 128 * h : 128 * h + 128]


def deinterleave(halves, i, out_ref):
    for h, half in enumerate(halves):
        for odd in range(2):
            rows = half[pl.ds(RANK * i + odd, RANK // 2, stride=2), :]
            start = RANK * i + RANK // 2 * odd
            out_ref[start : start + RANK // 2, 128 * h : 128 * h + 128] = rows.astype(bf16)


def prepare(*refs):
    for ref, parts in zip(refs[:2], (refs[2:4], refs[4:])):
        for part, value in zip(parts, split(ref[...])):
            part[...] = value


def compress(y_ref, test_high, test_low, ptest_high, ptest_low, basis_ref, w_ref, transfer_ref, a_ref, *halves):
    owned = y_ref.shape[1] // LEAF
    parents = owned // 2
    test = test_high[...], test_low[...]
    ys, ks, grams = [], [], []
    for i in range(owned):
        y = split(y_ref[:, LEAF * i : LEAF * i + LEAF])
        ys.append(y)
        k = split(product(test, y, (1, 0)))
        ks.append(k)
        grams.append(gram(k))
    linvs = inverses(grams)
    ptest = ptest_high[...], ptest_low[...]
    for i in range(owned):
        q = product(split(linvs[i]), ks[i], (1, 0))
        basis_ref[:, LEAF * i : LEAF * i + LEAF] = q
        keep(halves, i, product(split(q), ys[i], (1, 1)))
    blocks, stacks, grams = [], [], []
    for p in range(parents):
        stack = [h[2 * RANK * p : 2 * RANK * (p + 1), :] for h in halves]
        stack = split(jnp.concatenate(stack, axis=1))
        stacks.append(stack)
        c = split(product(ptest, stack, (1, 1)))
        blocks.append(c)
        grams.append(gram(c))
    for i in range(owned):
        deinterleave(halves, i, w_ref)
    finvs = inverses(grams)
    for p in range(parents):
        x = product(split(finvs[p]), blocks[p], (1, 0))
        transfer_ref[p] = x
        keep(halves, p, product(split(x), stacks[p], (1, 0)))
        deinterleave(halves, p, a_ref)


def project(o_ref, basis_ref, transfer_ref, v_ref, b_ref):
    owned = o_ref.shape[1] // LEAF
    for p in range(owned // 2):
        pair = []
        for i in (2 * p, 2 * p + 1):
            q = split(basis_ref[:, LEAF * i : LEAF * i + LEAF])
            v = product(q, split(o_ref[:, LEAF * i : LEAF * i + LEAF]), (1, 1))
            v_ref[RANK * i : RANK * i + RANK, :] = v.astype(bf16)
            pair.append(v)
        stack = split(jnp.concatenate(pair, axis=0))
        b_ref[RANK * p : RANK * p + RANK, :] = product(split(transfer_ref[p]), stack, (1, 0)).astype(bf16)


def couple(place, far_ref, count_ref, left_ref, *refs):
    pieces, out_ref, table = refs[:-2], refs[-2], refs[-1]
    rows = left_ref.shape[0] // RANK
    slots = far_ref.shape[1]
    at = 0
    for piece in pieces:
        size = piece.shape[0] // RANK
        for j in range(size):
            table[at + j] = piece[RANK * j : RANK * j + RANK, :]
        at += size
    lane = lax.broadcasted_iota(jnp.int32, (RANK // 2, 128), 1)
    low = lane < RANK
    samples = left_ref.shape[1]
    dims = (((1,), (1,)), ((), ()))
    spot = place()
    for i in range(rows):
        left = left_ref[RANK * i : RANK * i + RANK, :]
        for k in range(0, slots, 2):
            right = jnp.concatenate([table[jnp.clip(spot(far_ref[i, k + e]), 0, at - 1)] for e in range(2)], axis=0)
            x = lax.dot_general(left, right, dims, preferred_element_type=f32)
            even, odd = x[: RANK // 2], x[RANK // 2 :]
            first = jnp.where(low, even, pltpu.roll(odd, RANK, 1))
            second = jnp.where(low, pltpu.roll(even, RANK, 1), odd)
            for e, value in enumerate((first, second)):
                scale = jnp.where(k + e < count_ref[i], 1.0 / samples, 0.0).astype(f32)
                out_ref[pl.ds(i * 4 * RANK + k + e, RANK // 2, stride=8), :] = value * scale


vmem = pl.BlockSpec(memory_space=pltpu.VMEM)
smem = pl.BlockSpec(memory_space=pltpu.SMEM)
params = pltpu.CompilerParams(vmem_limit_bytes=16 << 20)


def cost(us):
    return pl.CostEstimate(flops=us * 10**9, bytes_accessed=us * 10**6, transcendentals=0)


def pack(x_ref, out_ref, sems):
    parts, _, width = out_ref.shape
    copies = [
        pltpu.make_async_copy(x_ref.at[:, width * c : width * c + width], out_ref.at[c], sems.at[c])
        for c in range(parts)
    ]
    for copy in copies:
        copy.start()
    for copy in copies:
        copy.wait()


def run_pack(x, parts):
    rows, columns = x.shape
    return pl.pallas_call(
        pack,
        out_shape=jax.ShapeDtypeStruct((parts, rows, columns // parts), f32),
        in_specs=[pl.BlockSpec(memory_space=pltpu.HBM)],
        out_specs=vmem,
        scratch_shapes=[pltpu.SemaphoreType.DMA((parts,))],
        compiler_params=params,
        cost_estimate=cost(1),
        name="pack",
    )(pltpu.with_memory_space_constraint(x, pltpu.HBM))


def run_prepare(test, ptest):
    return pl.pallas_call(
        prepare,
        out_shape=[jax.ShapeDtypeStruct(x.shape, bf16) for x in (test, test, ptest, ptest)],
        in_specs=[vmem] * 2,
        out_specs=[vmem] * 4,
        compiler_params=params,
        cost_estimate=cost(1),
        name="prepare",
    )(test, ptest)


def run_compress(y, tests):
    owned = y.shape[1] // LEAF
    samples = y.shape[0]
    return pl.pallas_call(
        compress,
        out_shape=(
            jax.ShapeDtypeStruct((RANK, y.shape[1]), f32),
            jax.ShapeDtypeStruct((owned * RANK, samples), bf16),
            jax.ShapeDtypeStruct((owned // 2, RANK, 2 * RANK), f32),
            jax.ShapeDtypeStruct((owned // 2 * RANK, samples), bf16),
        ),
        in_specs=[vmem] * 5,
        out_specs=(vmem,) * 4,
        scratch_shapes=[pltpu.VMEM((owned * RANK, 128), f32)] * (samples // 128),
        compiler_params=params,
        cost_estimate=cost(12),
        name="compress",
    )(y, *tests)


def run_project(o, basis, transfer):
    owned = o.shape[1] // LEAF
    samples = o.shape[0]
    return pl.pallas_call(
        project,
        out_shape=(
            jax.ShapeDtypeStruct((owned * RANK, samples), bf16),
            jax.ShapeDtypeStruct((owned // 2 * RANK, samples), bf16),
        ),
        in_specs=[vmem] * 3,
        out_specs=(vmem,) * 2,
        compiler_params=params,
        cost_estimate=cost(4),
        name="project",
    )(o, basis, transfer)


def run_couple(place, far, count, left, pieces):
    rows, slots = far.shape
    total = sum(p.shape[0] for p in pieces) // RANK
    out = pl.pallas_call(
        functools.partial(couple, place),
        out_shape=jax.ShapeDtypeStruct((rows * 4 * RANK, 128), f32),
        in_specs=[smem, smem, vmem] + [vmem] * len(pieces),
        out_specs=vmem,
        scratch_shapes=[pltpu.VMEM((total, RANK, left.shape[1]), bf16)],
        compiler_params=params,
        cost_estimate=cost(3),
    )(far, count, left, *pieces)
    out = out.reshape(rows, RANK // 2, slots, 128)
    return out.transpose(0, 2, 1, 3).reshape(rows, slots, RANK * RANK)


def gathered(array):
    devices = lax.axis_size("samp")
    rows, columns = array.shape
    sent = (run_pack(array, devices) * SCALE).astype(jnp.float16)
    got = lax.all_to_all(sent, "samp", split_axis=0, concat_axis=0, tiled=True)
    return got.astype(f32).reshape(rows * devices, columns // devices) * (1.0 / SCALE)


def swaps(chain, late):
    found = []
    for i, j in list(zip(chain, chain[1:]))[late::2]:
        found += [(i, j), (j, i)]
    return found


def near_pairs(size):
    return swaps(range(size), 1), swaps(range(size), 0)


def far_pairs(rows):
    sets = [sum((swaps(range(start, rows, 3), late) for start in range(3)), []) for late in (1, 0)]
    sets[0] += [(1, 2)]
    sets[1] += [(rows - 2, rows - 3)]
    got = [{r} for r in range(rows)]
    for pairs in sets:
        assert len({i for i, _ in pairs}) == len({j for _, j in pairs}) == len(pairs)
        for i, j in pairs:
            got[j] |= {i - 1, i, i + 1}
    for r in range(rows):
        have = got[r] | {r - 1, r + 1}
        assert all(q in have for q in range(max(r - REACH, 0), min(r + REACH + 1, rows)))
    return sets


def body(sketch, probes, test_leaf, test_parent, leaf_far, leaf_count, parent_far, parent_count):
    owned = leaf_far.shape[0]
    per_device = parent_far.shape[0]
    row_count = lax.axis_size("rows")
    samp_count = lax.axis_size("samp")
    y = gathered(sketch)
    o = gathered(probes)
    tests = run_prepare(test_leaf, test_parent)
    basis, w, transfer, a = run_compress(y, tests)
    v, b = run_project(o, basis, transfer)
    pairs = near_pairs(row_count)
    near = [b] + [lax.ppermute(b, "rows", pairs[e]) for e in range(2)]
    near = jnp.concatenate(near, axis=0)
    both = ("rows", "samp")
    pairs = near_pairs(row_count * samp_count)
    halo = [v] + [lax.ppermute(v, both, pairs[e]) for e in range(2)]
    pairs = far_pairs(row_count)
    far = [lax.ppermute(near, "rows", pairs[e]) for e in range(2)]

    def leaf_place():
        own = lax.axis_index(both)
        first = own * owned
        odd = lax.rem(own, 2)

        def spot(leaf):
            later = (leaf >= first + owned).astype(jnp.int32)
            earlier = (leaf < first).astype(jnp.int32)
            piece = later * (2 - odd) + earlier * (1 + odd)
            return leaf - first + (earlier - later + piece) * owned

        return spot

    def parent_place():
        row = lax.axis_index("rows")
        behind = lax.rem(lax.div(row, 3), 2) == 0
        one = jnp.where(behind, -(REACH - 1), REACH - 1)
        two = -one
        one = jnp.where(row == 2, -1, one)
        two = jnp.where(row == row_count - 3, 1, two)
        across = per_device * samp_count

        def spot(parent):
            away = lax.div(parent, across) - row

            def among(there, centre):
                odd_there = lax.rem(row + centre + 2 * REACH, 2)
                return jnp.where(there == 0, 0, jnp.where((there == 1) == (odd_there == 1), 1, 2))

            far_at = jnp.where(abs(away - one) <= 1, 3 + among(away - one, one), 6 + among(away - two, two))
            at = jnp.where(abs(away) <= 1, among(away, 0), far_at)
            return at * per_device + lax.rem(parent, per_device)

        return spot

    leaf_coupling = run_couple(leaf_place, leaf_far, leaf_count, w, halo)
    parent_coupling = run_couple(parent_place, parent_far, parent_count, a, [near, *far])
    return (basis, leaf_coupling, transfer, parent_coupling)


def solution(mesh):
    return jax.shard_map(
        body,
        mesh=mesh,
        in_specs=(
            P("samp", "rows"),
            P("samp", "rows"),
            P(),
            P(),
            P(("rows", "samp"), None),
            P(("rows", "samp")),
            P(("rows", "samp"), None),
            P(("rows", "samp")),
        ),
        out_specs=(
            P(None, ("rows", "samp")),
            P(("rows", "samp"), None, None),
            P(("rows", "samp"), None, None),
            P(("rows", "samp"), None, None),
        ),
        check_vma=False,
    )
```

```python
import functools
import jax
import jax.numpy as jnp
from jax import lax
from jax.experimental import pallas as pl
from jax.experimental.pallas import tpu as pltpu
from jax.sharding import PartitionSpec as P


f32 = jnp.float32
bf16 = jnp.bfloat16

LEAF = 256
RANK = 64
REACH = 4
SCALE = 8192.0


def split(x):
    high = x.astype(bf16)
    low = (x - high.astype(f32)).astype(bf16)
    return high, low


def product(a, b, contract):
    dims = ((contract[0],), (contract[1],)), ((), ())
    dot = functools.partial(lax.dot_general, dimension_numbers=dims, preferred_element_type=f32)
    rows = a[0].shape[0]
    both = dot(jnp.concatenate(a, axis=0), b[0])
    return both[:rows] + (both[rows:] + dot(a[0], b[1]))


def gram(a):
    both = jnp.concatenate(a, axis=0)
    rows = a[0].shape[0]
    dims = (((1,), (1,)), ((), ()))
    full = lax.dot_general(both, both, dims, preferred_element_type=f32)
    total = full[:rows] + full[rows:]
    return total[:, :rows] + total[:, rows:]


def inverse_factors(packs):
    tiles = RANK // 8
    lane = lax.broadcasted_iota(jnp.int32, (8, 128), 1)
    sub = lax.broadcasted_iota(jnp.int32, (8, 128), 0)
    column = lane % RANK
    half = lane - column

    def row(x, k):
        return jnp.broadcast_to(x[k : k + 1, :], (8, 128))

    state = [[p[8 * t : 8 * t + 8, :] for t in range(tiles)] for p in packs]
    for block in range(tiles):
        start = 8 * block
        cols = [
            [
                [jnp.take_along_axis(s[t], half + (start + k), axis=1) for t in range(block, tiles)]
                for k in range(8)
            ]
            for s in state
        ]
        inside = (column >= start) & (column < start + 8)
        unit = jnp.where(column == start + sub, 1.0, 0.0).astype(f32)
        for s, c in zip(state, cols):
            head = jnp.where(inside, unit, s[block])
            rest = [jnp.where(inside, 0.0, s[t]) for t in range(block + 1, tiles)]
            pivots = jnp.ones((8, 128), f32)
            for k in range(8):
                pivot = row(c[k][0], k)
                pivots = jnp.where(sub == k, pivot, pivots)
                inv = 1.0 / pivot
                mult = [x * inv for x in c[k]]
                mult[0] = jnp.where(sub > k, mult[0], 0.0)
                for k2 in range(k + 1, 8):
                    factor = row(c[k][0], k2)
                    c[k2] = [x - m * factor for x, m in zip(c[k2], mult)]
                lead = row(head, k)
                head = head - mult[0] * lead
                rest = [x - m * lead for x, m in zip(rest, mult[1:])]
            head = head * lax.rsqrt(pivots)
            s[block] = jnp.where(column <= start + sub, head, 0.0)
            s[block + 1 :] = rest
    return [jnp.concatenate(s, axis=0) for s in state]


def inverses(grams):
    padded = list(grams) + ([grams[-1]] if len(grams) % 2 else [])
    packs = [jnp.concatenate(padded[i : i + 2], axis=1) for i in range(0, len(padded), 2)]
    done = inverse_factors(packs)
    out = []
    for p in done:
        out += [p[:, :RANK], p[:, RANK:]]
    return out[: len(grams)]


def keep(halves, i, value):
    for h, half in enumerate(halves):
        half[RANK * i : RANK * i + RANK, :] = value[:, 128 * h : 128 * h + 128]


def deinterleave(halves, i, out_ref):
    for h, half in enumerate(halves):
        for odd in range(2):
            rows = half[pl.ds(RANK * i + odd, RANK // 2, stride=2), :]
            start = RANK * i + RANK // 2 * odd
            out_ref[start : start + RANK // 2, 128 * h : 128 * h + 128] = rows.astype(bf16)


def prepare(*refs):
    for ref, parts in zip(refs[:2], (refs[2:4], refs[4:])):
        for part, value in zip(parts, split(ref[...])):
            part[...] = value


def compress(y_ref, test_high, test_low, ptest_high, ptest_low, basis_ref, w_ref, transfer_ref, a_ref, *halves):
    owned = y_ref.shape[1] // LEAF
    parents = owned // 2
    test = test_high[...], test_low[...]
    ys, ks, grams = [], [], []
    for i in range(owned):
        y = split(y_ref[:, LEAF * i : LEAF * i + LEAF])
        ys.append(y)
        k = split(product(test, y, (1, 0)))
        ks.append(k)
        grams.append(gram(k))
    linvs = inverses(grams)
    ptest = ptest_high[...], ptest_low[...]
    for i in range(owned):
        q = product(split(linvs[i]), ks[i], (1, 0))
        basis_ref[:, LEAF * i : LEAF * i + LEAF] = q
        keep(halves, i, product(split(q), ys[i], (1, 1)))
    blocks, stacks, grams = [], [], []
    for p in range(parents):
        stack = [h[2 * RANK * p : 2 * RANK * (p + 1), :] for h in halves]
        stack = split(jnp.concatenate(stack, axis=1))
        stacks.append(stack)
        c = split(product(ptest, stack, (1, 1)))
        blocks.append(c)
        grams.append(gram(c))
    for i in range(owned):
        deinterleave(halves, i, w_ref)
    finvs = inverses(grams)
    for p in range(parents):
        x = product(split(finvs[p]), blocks[p], (1, 0))
        transfer_ref[p] = x
        keep(halves, p, product(split(x), stacks[p], (1, 0)))
        deinterleave(halves, p, a_ref)


def project(o_ref, basis_ref, transfer_ref, v_ref, b_ref):
    owned = o_ref.shape[1] // LEAF
    for p in range(owned // 2):
        pair = []
        for i in (2 * p, 2 * p + 1):
            q = split(basis_ref[:, LEAF * i : LEAF * i + LEAF])
            v = product(q, split(o_ref[:, LEAF * i : LEAF * i + LEAF]), (1, 1))
            v_ref[RANK * i : RANK * i + RANK, :] = v.astype(bf16)
            pair.append(v)
        stack = split(jnp.concatenate(pair, axis=0))
        b_ref[RANK * p : RANK * p + RANK, :] = product(split(transfer_ref[p]), stack, (1, 0)).astype(bf16)


def couple(place, far_ref, count_ref, left_ref, *refs):
    pieces, (out_ref, table, stage, sems) = refs[:-4], refs[-4:]
    rows = left_ref.shape[0] // RANK
    slots = far_ref.shape[1]
    at = 0
    for piece in pieces:
        size = piece.shape[0] // RANK
        for j in range(size):
            table[at + j] = piece[RANK * j : RANK * j + RANK, :]
        at += size
    lane = lax.broadcasted_iota(jnp.int32, (RANK // 2, 128), 1)
    low = lane < RANK
    samples = left_ref.shape[1]
    dims = (((1,), (1,)), ((), ()))
    spot = place()
    copies = []
    for i in range(rows):
        left = left_ref[RANK * i : RANK * i + RANK, :]
        for k in range(0, slots, 2):
            right = jnp.concatenate([table[jnp.clip(spot(far_ref[i, k + e]), 0, at - 1)] for e in range(2)], axis=0)
            x = lax.dot_general(left, right, dims, preferred_element_type=f32)
            even, odd = x[: RANK // 2], x[RANK // 2 :]
            first = jnp.where(low, even, pltpu.roll(odd, RANK, 1))
            second = jnp.where(low, pltpu.roll(even, RANK, 1), odd)
            for e, value in enumerate((first, second)):
                scale = jnp.where(k + e < count_ref[i], 1.0 / samples, 0.0).astype(f32)
                stage[pl.ds(i * 4 * RANK + k + e, RANK // 2, stride=8), :] = value * scale
        done = pl.ds(i * 4 * RANK, 4 * RANK)
        copies.append(pltpu.make_async_copy(stage.at[done, :], out_ref.at[done, :], sems.at[i]))
        copies[i].start()
    for copy in copies:
        copy.wait()


vmem = pl.BlockSpec(memory_space=pltpu.VMEM)
smem = pl.BlockSpec(memory_space=pltpu.SMEM)
params = pltpu.CompilerParams(vmem_limit_bytes=16 << 20)


def cost(us):
    return pl.CostEstimate(flops=us * 10**9, bytes_accessed=us * 10**6, transcendentals=0)


def pack(x_ref, out_ref, sems):
    parts, _, width = out_ref.shape
    copies = [
        pltpu.make_async_copy(x_ref.at[:, width * c : width * c + width], out_ref.at[c], sems.at[c])
        for c in range(parts)
    ]
    for copy in copies:
        copy.start()
    for copy in copies:
        copy.wait()


def run_pack(x, parts):
    rows, columns = x.shape
    return pl.pallas_call(
        pack,
        out_shape=jax.ShapeDtypeStruct((parts, rows, columns // parts), f32),
        in_specs=[pl.BlockSpec(memory_space=pltpu.HBM)],
        out_specs=vmem,
        scratch_shapes=[pltpu.SemaphoreType.DMA((parts,))],
        compiler_params=params,
        cost_estimate=cost(1),
        name="pack",
    )(pltpu.with_memory_space_constraint(x, pltpu.HBM))


def run_prepare(test, ptest):
    return pl.pallas_call(
        prepare,
        out_shape=[jax.ShapeDtypeStruct(x.shape, bf16) for x in (test, test, ptest, ptest)],
        in_specs=[vmem] * 2,
        out_specs=[vmem] * 4,
        compiler_params=params,
        cost_estimate=cost(1),
        name="prepare",
    )(test, ptest)


def run_compress(y, tests):
    owned = y.shape[1] // LEAF
    samples = y.shape[0]
    return pl.pallas_call(
        compress,
        out_shape=(
            jax.ShapeDtypeStruct((RANK, y.shape[1]), f32),
            jax.ShapeDtypeStruct((owned * RANK, samples), bf16),
            jax.ShapeDtypeStruct((owned // 2, RANK, 2 * RANK), f32),
            jax.ShapeDtypeStruct((owned // 2 * RANK, samples), bf16),
        ),
        in_specs=[vmem] * 5,
        out_specs=(vmem,) * 4,
        scratch_shapes=[pltpu.VMEM((owned * RANK, 128), f32)] * (samples // 128),
        compiler_params=params,
        cost_estimate=cost(12),
        name="compress",
    )(y, *tests)


def run_project(o, basis, transfer):
    owned = o.shape[1] // LEAF
    samples = o.shape[0]
    return pl.pallas_call(
        project,
        out_shape=(
            jax.ShapeDtypeStruct((owned * RANK, samples), bf16),
            jax.ShapeDtypeStruct((owned // 2 * RANK, samples), bf16),
        ),
        in_specs=[vmem] * 3,
        out_specs=(vmem,) * 2,
        compiler_params=params,
        cost_estimate=cost(4),
        name="project",
    )(o, basis, transfer)


def run_couple(place, far, count, left, pieces):
    rows, slots = far.shape
    total = sum(p.shape[0] for p in pieces) // RANK
    out = pl.pallas_call(
        functools.partial(couple, place),
        out_shape=jax.ShapeDtypeStruct((rows * 4 * RANK, 128), f32),
        in_specs=[smem, smem, vmem] + [vmem] * len(pieces),
        out_specs=pl.BlockSpec(memory_space=pl.ANY),
        scratch_shapes=[
            pltpu.VMEM((total, RANK, left.shape[1]), bf16),
            pltpu.VMEM((rows * 4 * RANK, 128), f32),
            pltpu.SemaphoreType.DMA((rows,)),
        ],
        compiler_params=params,
        cost_estimate=cost(3),
    )(far, count, left, *pieces)
    out = out.reshape(rows, RANK // 2, slots, 128)
    return out.transpose(0, 2, 1, 3).reshape(rows, slots, RANK * RANK)


def gathered(array):
    devices = lax.axis_size("samp")
    rows, columns = array.shape
    sent = (run_pack(array, devices) * SCALE).astype(jnp.float16)
    got = lax.all_to_all(sent, "samp", split_axis=0, concat_axis=0, tiled=True)
    return got.astype(f32).reshape(rows * devices, columns // devices) * (1.0 / SCALE)


def swaps(chain, late):
    found = []
    for i, j in list(zip(chain, chain[1:]))[late::2]:
        found += [(i, j), (j, i)]
    return found


def near_pairs(size):
    return swaps(range(size), 1), swaps(range(size), 0)


def far_pairs(rows):
    sets = [[], []]
    for start in range(3):
        for late in range(2):
            sets[late ^ (start != 1)] += swaps(range(start, rows, 3), late)
    sets[0] += [(0, 2), (rows - 1, rows - 3)]
    got = [{r} for r in range(rows)]
    for pairs in sets:
        assert len({i for i, _ in pairs}) == len({j for _, j in pairs}) == len(pairs)
        for i, j in pairs:
            got[j] |= {i - 1, i, i + 1}
    for r in range(rows):
        have = got[r] | {r - 1, r + 1}
        assert all(q in have for q in range(max(r - REACH, 0), min(r + REACH + 1, rows)))
    return sets


def body(sketch, probes, test_leaf, test_parent, leaf_far, leaf_count, parent_far, parent_count):
    owned = leaf_far.shape[0]
    per_device = parent_far.shape[0]
    row_count = lax.axis_size("rows")
    samp_count = lax.axis_size("samp")
    y = gathered(sketch)
    o = gathered(probes)
    tests = run_prepare(test_leaf, test_parent)
    basis, w, transfer, a = run_compress(y, tests)
    v, b = run_project(o, basis, transfer)
    pairs = near_pairs(row_count)
    near = [b] + [lax.ppermute(b, "rows", pairs[e]) for e in range(2)]
    near = jnp.concatenate(near, axis=0)
    both = ("rows", "samp")
    pairs = near_pairs(row_count * samp_count)
    halo = [v] + [lax.ppermute(v, both, pairs[e]) for e in range(2)]
    pairs = far_pairs(row_count)
    far = [lax.ppermute(near, "rows", pairs[e]) for e in range(2)]

    def leaf_place():
        own = lax.axis_index(both)
        first = own * owned
        odd = lax.rem(own, 2)

        def spot(leaf):
            later = (leaf >= first + owned).astype(jnp.int32)
            earlier = (leaf < first).astype(jnp.int32)
            piece = later * (2 - odd) + earlier * (1 + odd)
            return leaf - first + (earlier - later + piece) * owned

        return spot

    def parent_place():
        row = lax.axis_index("rows")
        behind = (lax.rem(lax.div(row, 3), 2) == 0) != (lax.rem(row, 3) == 1)
        one = jnp.where(behind, -(REACH - 1), REACH - 1)
        two = -one
        one = jnp.where(row == 2, -2, one)
        one = jnp.where(row == row_count - 3, 2, one)
        across = per_device * samp_count

        def spot(parent):
            away = lax.div(parent, across) - row

            def among(there, centre):
                odd_there = lax.rem(row + centre + 2 * REACH, 2)
                return jnp.where(there == 0, 0, jnp.where((there == 1) == (odd_there == 1), 1, 2))

            far_at = jnp.where(abs(away - one) <= 1, 3 + among(away - one, one), 6 + among(away - two, two))
            at = jnp.where(abs(away) <= 1, among(away, 0), far_at)
            return at * per_device + lax.rem(parent, per_device)

        return spot

    leaf_coupling = run_couple(leaf_place, leaf_far, leaf_count, w, halo)
    parent_coupling = run_couple(parent_place, parent_far, parent_count, a, [near, *far])
    return (basis, leaf_coupling, transfer, parent_coupling)


def solution(mesh):
    return jax.shard_map(
        body,
        mesh=mesh,
        in_specs=(
            P("samp", "rows"),
            P("samp", "rows"),
            P(),
            P(),
            P(("rows", "samp"), None),
            P(("rows", "samp")),
            P(("rows", "samp"), None),
            P(("rows", "samp")),
        ),
        out_specs=(
            P(None, ("rows", "samp")),
            P(("rows", "samp"), None, None),
            P(("rows", "samp"), None, None),
            P(("rows", "samp"), None, None),
        ),
        check_vma=False,
    )
```

```python
import functools
import jax
import jax.numpy as jnp
from jax import lax
from jax.experimental import pallas as pl
from jax.experimental.pallas import tpu as pltpu
from jax.sharding import PartitionSpec as P


f32 = jnp.float32
bf16 = jnp.bfloat16

LEAF = 256
RANK = 64
REACH = 4
SCALE = 8192.0


def split(x):
    high = x.astype(bf16)
    low = (x - high.astype(f32)).astype(bf16)
    return high, low


def product(a, b, contract):
    dims = ((contract[0],), (contract[1],)), ((), ())
    dot = functools.partial(lax.dot_general, dimension_numbers=dims, preferred_element_type=f32)
    rows = a[0].shape[0]
    both = dot(jnp.concatenate(a, axis=0), b[0])
    return both[:rows] + (both[rows:] + dot(a[0], b[1]))


def gram(a):
    both = jnp.concatenate(a, axis=0)
    rows = a[0].shape[0]
    dims = (((1,), (1,)), ((), ()))
    full = lax.dot_general(both, both, dims, preferred_element_type=f32)
    total = full[:rows] + full[rows:]
    return total[:, :rows] + total[:, rows:]


def inverse_factors(packs):
    tiles = RANK // 8
    lane = lax.broadcasted_iota(jnp.int32, (8, 128), 1)
    sub = lax.broadcasted_iota(jnp.int32, (8, 128), 0)
    column = lane % RANK
    half = lane - column

    def row(x, k):
        return jnp.broadcast_to(x[k : k + 1, :], (8, 128))

    state = [[p[8 * t : 8 * t + 8, :] for t in range(tiles)] for p in packs]
    for block in range(tiles):
        start = 8 * block
        cols = [
            [
                [jnp.take_along_axis(s[t], half + (start + k), axis=1) for t in range(block, tiles)]
                for k in range(8)
            ]
            for s in state
        ]
        inside = (column >= start) & (column < start + 8)
        unit = jnp.where(column == start + sub, 1.0, 0.0).astype(f32)
        for s, c in zip(state, cols):
            head = jnp.where(inside, unit, s[block])
            rest = [jnp.where(inside, 0.0, s[t]) for t in range(block + 1, tiles)]
            pivots = jnp.ones((8, 128), f32)
            for k in range(8):
                pivot = row(c[k][0], k)
                pivots = jnp.where(sub == k, pivot, pivots)
                inv = 1.0 / pivot
                mult = [x * inv for x in c[k]]
                mult[0] = jnp.where(sub > k, mult[0], 0.0)
                for k2 in range(k + 1, 8):
                    factor = row(c[k][0], k2)
                    c[k2] = [x - m * factor for x, m in zip(c[k2], mult)]
                lead = row(head, k)
                head = head - mult[0] * lead
                rest = [x - m * lead for x, m in zip(rest, mult[1:])]
            head = head * lax.rsqrt(pivots)
            s[block] = jnp.where(column <= start + sub, head, 0.0)
            s[block + 1 :] = rest
    return [jnp.concatenate(s, axis=0) for s in state]


def inverses(grams):
    padded = list(grams) + ([grams[-1]] if len(grams) % 2 else [])
    packs = [jnp.concatenate(padded[i : i + 2], axis=1) for i in range(0, len(padded), 2)]
    done = inverse_factors(packs)
    out = []
    for p in done:
        out += [p[:, :RANK], p[:, RANK:]]
    return out[: len(grams)]


def keep(halves, i, value):
    for h, half in enumerate(halves):
        half[RANK * i : RANK * i + RANK, :] = value[:, 128 * h : 128 * h + 128]


def deinterleave(halves, i, out_ref):
    for h, half in enumerate(halves):
        for odd in range(2):
            rows = half[pl.ds(RANK * i + odd, RANK // 2, stride=2), :]
            start = RANK * i + RANK // 2 * odd
            out_ref[start : start + RANK // 2, 128 * h : 128 * h + 128] = rows.astype(bf16)


def prepare(*refs):
    for ref, parts in zip(refs[:2], (refs[2:4], refs[4:])):
        for part, value in zip(parts, split(ref[...])):
            part[...] = value


def compress(y_ref, test_high, test_low, ptest_high, ptest_low, basis_ref, w_ref, transfer_ref, a_ref, *halves):
    owned = y_ref.shape[1] // LEAF
    parents = owned // 2
    test = test_high[...], test_low[...]
    ys, ks, grams = [], [], []
    for i in range(owned):
        y = split(y_ref[:, LEAF * i : LEAF * i + LEAF])
        ys.append(y)
        k = split(product(test, y, (1, 0)))
        ks.append(k)
        grams.append(gram(k))
    linvs = inverses(grams)
    ptest = ptest_high[...], ptest_low[...]
    for i in range(owned):
        q = product(split(linvs[i]), ks[i], (1, 0))
        basis_ref[:, LEAF * i : LEAF * i + LEAF] = q
        keep(halves, i, product(split(q), ys[i], (1, 1)))
    blocks, stacks, grams = [], [], []
    for p in range(parents):
        stack = [h[2 * RANK * p : 2 * RANK * (p + 1), :] for h in halves]
        stack = split(jnp.concatenate(stack, axis=1))
        stacks.append(stack)
        c = split(product(ptest, stack, (1, 1)))
        blocks.append(c)
        grams.append(gram(c))
    for i in range(owned):
        deinterleave(halves, i, w_ref)
    finvs = inverses(grams)
    for p in range(parents):
        x = product(split(finvs[p]), blocks[p], (1, 0))
        transfer_ref[p] = x
        keep(halves, p, product(split(x), stacks[p], (1, 0)))
        deinterleave(halves, p, a_ref)


def project(o_ref, basis_ref, transfer_ref, v_ref, b_ref):
    owned = o_ref.shape[1] // LEAF
    for p in range(owned // 2):
        pair = []
        for i in (2 * p, 2 * p + 1):
            q = split(basis_ref[:, LEAF * i : LEAF * i + LEAF])
            v = product(q, split(o_ref[:, LEAF * i : LEAF * i + LEAF]), (1, 1))
            v_ref[RANK * i : RANK * i + RANK, :] = v.astype(bf16)
            pair.append(v)
        stack = split(jnp.concatenate(pair, axis=0))
        b_ref[RANK * p : RANK * p + RANK, :] = product(split(transfer_ref[p]), stack, (1, 0)).astype(bf16)


def couple(place, far_ref, count_ref, left_ref, *refs):
    pieces, (out_ref, table, stage, sems) = refs[:-4], refs[-4:]
    rows = left_ref.shape[0] // RANK
    slots = far_ref.shape[1]
    at = 0
    for piece in pieces:
        size = piece.shape[0] // RANK
        for j in range(size):
            table[at + j] = piece[RANK * j : RANK * j + RANK, :]
        at += size
    lane = lax.broadcasted_iota(jnp.int32, (RANK // 2, 128), 1)
    low = lane < RANK
    samples = left_ref.shape[1]
    dims = (((1,), (1,)), ((), ()))
    spot = place()
    copies = []
    for i in range(rows):
        left = left_ref[RANK * i : RANK * i + RANK, :]
        for k in range(0, slots, 2):
            right = jnp.concatenate([table[jnp.clip(spot(far_ref[i, k + e]), 0, at - 1)] for e in range(2)], axis=0)
            x = lax.dot_general(left, right, dims, preferred_element_type=f32)
            even, odd = x[: RANK // 2], x[RANK // 2 :]
            first = jnp.where(low, even, pltpu.roll(odd, RANK, 1))
            second = jnp.where(low, pltpu.roll(even, RANK, 1), odd)
            for e, value in enumerate((first, second)):
                scale = jnp.where(k + e < count_ref[i], 1.0 / samples, 0.0).astype(f32)
                stage[pl.ds(i * 4 * RANK + k + e, RANK // 2, stride=8), :] = value * scale
        done = pl.ds(i * 4 * RANK, 4 * RANK)
        copies.append(pltpu.make_async_copy(stage.at[done, :], out_ref.at[done, :], sems.at[i]))
        copies[i].start()
    for copy in copies:
        copy.wait()


vmem = pl.BlockSpec(memory_space=pltpu.VMEM)
smem = pl.BlockSpec(memory_space=pltpu.SMEM)
params = pltpu.CompilerParams(vmem_limit_bytes=16 << 20)


def cost(us):
    return pl.CostEstimate(flops=us * 10**9, bytes_accessed=us * 10**6, transcendentals=0)


def pack(x_ref, out_ref, sems):
    parts, _, width = out_ref.shape
    copies = [
        pltpu.make_async_copy(x_ref.at[:, width * c : width * c + width], out_ref.at[c], sems.at[c])
        for c in range(parts)
    ]
    for copy in copies:
        copy.start()
    for copy in copies:
        copy.wait()


def run_pack(x, parts):
    rows, columns = x.shape
    return pl.pallas_call(
        pack,
        out_shape=jax.ShapeDtypeStruct((parts, rows, columns // parts), f32),
        in_specs=[pl.BlockSpec(memory_space=pltpu.HBM)],
        out_specs=vmem,
        scratch_shapes=[pltpu.SemaphoreType.DMA((parts,))],
        compiler_params=params,
        cost_estimate=cost(1),
        name="pack",
    )(pltpu.with_memory_space_constraint(x, pltpu.HBM))


def run_prepare(test, ptest):
    return pl.pallas_call(
        prepare,
        out_shape=[jax.ShapeDtypeStruct(x.shape, bf16) for x in (test, test, ptest, ptest)],
        in_specs=[vmem] * 2,
        out_specs=[vmem] * 4,
        compiler_params=params,
        cost_estimate=cost(1),
        name="prepare",
    )(test, ptest)


def run_compress(y, tests):
    owned = y.shape[1] // LEAF
    samples = y.shape[0]
    return pl.pallas_call(
        compress,
        out_shape=(
            jax.ShapeDtypeStruct((RANK, y.shape[1]), f32),
            jax.ShapeDtypeStruct((owned * RANK, samples), bf16),
            jax.ShapeDtypeStruct((owned // 2, RANK, 2 * RANK), f32),
            jax.ShapeDtypeStruct((owned // 2 * RANK, samples), bf16),
        ),
        in_specs=[vmem] * 5,
        out_specs=(vmem,) * 4,
        scratch_shapes=[pltpu.VMEM((owned * RANK, 128), f32)] * (samples // 128),
        compiler_params=params,
        cost_estimate=cost(12),
        name="compress",
    )(y, *tests)


def run_project(o, basis, transfer):
    owned = o.shape[1] // LEAF
    samples = o.shape[0]
    return pl.pallas_call(
        project,
        out_shape=(
            jax.ShapeDtypeStruct((owned * RANK, samples), bf16),
            jax.ShapeDtypeStruct((owned // 2 * RANK, samples), bf16),
        ),
        in_specs=[vmem] * 3,
        out_specs=(vmem,) * 2,
        compiler_params=params,
        cost_estimate=cost(4),
        name="project",
    )(o, basis, transfer)


def run_couple(place, far, count, left, pieces):
    rows, slots = far.shape
    total = sum(p.shape[0] for p in pieces) // RANK
    out = pl.pallas_call(
        functools.partial(couple, place),
        out_shape=jax.ShapeDtypeStruct((rows * 4 * RANK, 128), f32),
        in_specs=[smem, smem, vmem] + [vmem] * len(pieces),
        out_specs=pl.BlockSpec(memory_space=pl.ANY),
        scratch_shapes=[
            pltpu.VMEM((total, RANK, left.shape[1]), bf16),
            pltpu.VMEM((rows * 4 * RANK, 128), f32),
            pltpu.SemaphoreType.DMA((rows,)),
        ],
        compiler_params=params,
        cost_estimate=cost(3),
    )(far, count, left, *pieces)
    out = out.reshape(rows, RANK // 2, slots, 128)
    return out.transpose(0, 2, 1, 3).reshape(rows, slots, RANK * RANK)


def gathered(array):
    devices = lax.axis_size("samp")
    rows, columns = array.shape
    sent = (run_pack(array, devices) * SCALE).astype(jnp.float16)
    got = lax.all_to_all(sent, "samp", split_axis=0, concat_axis=0, tiled=True)
    return got.astype(f32).reshape(rows * devices, columns // devices) * (1.0 / SCALE)


def swaps(chain, late):
    found = []
    for i, j in list(zip(chain, chain[1:]))[late::2]:
        found += [(i, j), (j, i)]
    return found


def near_pairs(size):
    return swaps(range(size), 1), swaps(range(size), 0)


def far_pairs(rows):
    sets = [sum((swaps(range(start, rows, 3), late) for start in range(3)), []) for late in (1, 0)]
    edge = [(0, 2), (rows - 1, rows - 3)]
    got = [{r} for r in range(rows)]
    for pairs in sets:
        assert len({i for i, _ in pairs}) == len({j for _, j in pairs}) == len(pairs)
        for i, j in pairs:
            got[j] |= {i - 1, i, i + 1}
    for i, j in edge:
        got[j] |= {i}
    for r in range(rows):
        have = got[r] | {r - 1, r + 1}
        assert all(q in have for q in range(max(r - REACH, 0), min(r + REACH + 1, rows)))
    return *sets, edge


def body(sketch, probes, test_leaf, test_parent, leaf_far, leaf_count, parent_far, parent_count):
    owned = leaf_far.shape[0]
    per_device = parent_far.shape[0]
    row_count = lax.axis_size("rows")
    samp_count = lax.axis_size("samp")
    y = gathered(sketch)
    o = gathered(probes)
    tests = run_prepare(test_leaf, test_parent)
    basis, w, transfer, a = run_compress(y, tests)
    v, b = run_project(o, basis, transfer)
    pairs = near_pairs(row_count)
    near = [b] + [lax.ppermute(b, "rows", pairs[e]) for e in range(2)]
    near = jnp.concatenate(near, axis=0)
    both = ("rows", "samp")
    pairs = near_pairs(row_count * samp_count)
    halo = [v] + [lax.ppermute(v, both, pairs[e]) for e in range(2)]
    pairs = far_pairs(row_count)
    far = [lax.ppermute(near, "rows", pairs[e]) for e in range(2)]
    edge = lax.ppermute(b, "rows", pairs[2])

    def leaf_place():
        own = lax.axis_index(both)
        first = own * owned
        odd = lax.rem(own, 2)

        def spot(leaf):
            later = (leaf >= first + owned).astype(jnp.int32)
            earlier = (leaf < first).astype(jnp.int32)
            piece = later * (2 - odd) + earlier * (1 + odd)
            return leaf - first + (earlier - later + piece) * owned

        return spot

    def parent_place():
        row = lax.axis_index("rows")
        behind = lax.rem(lax.div(row, 3), 2) == 0
        one = jnp.where(behind, -(REACH - 1), REACH - 1)
        two = -one
        last = row_count - 1
        across = per_device * samp_count

        def spot(parent):
            away = lax.div(parent, across) - row

            def among(there, centre):
                odd_there = lax.rem(row + centre + 2 * REACH, 2)
                return jnp.where(there == 0, 0, jnp.where((there == 1) == (odd_there == 1), 1, 2))

            far_at = jnp.where(abs(away - one) <= 1, 3 + among(away - one, one), 6 + among(away - two, two))
            at = jnp.where(abs(away) <= 1, among(away, 0), far_at)
            beyond = ((row == 2) & (away == -2)) | ((row == last - 2) & (away == 2))
            at = jnp.where(beyond, 9, at)
            return at * per_device + lax.rem(parent, per_device)

        return spot

    leaf_coupling = run_couple(leaf_place, leaf_far, leaf_count, w, halo)
    parent_coupling = run_couple(parent_place, parent_far, parent_count, a, [near, *far, edge])
    return (basis, leaf_coupling, transfer, parent_coupling)


def solution(mesh):
    return jax.shard_map(
        body,
        mesh=mesh,
        in_specs=(
            P("samp", "rows"),
            P("samp", "rows"),
            P(),
            P(),
            P(("rows", "samp"), None),
            P(("rows", "samp")),
            P(("rows", "samp"), None),
            P(("rows", "samp")),
        ),
        out_specs=(
            P(None, ("rows", "samp")),
            P(("rows", "samp"), None, None),
            P(("rows", "samp"), None, None),
            P(("rows", "samp"), None, None),
        ),
        check_vma=False,
    )
```
